32 devices in a mesh: pipe: 8 (over y, x, core), tensor: 4 (over z).
Axes of the slice: x: 2, y: 2, z: 4, core: 2. Of those that a mesh axis runs over, the one named last changes fastest.
Arguments:
- fwd_inputs: bfloat16 [8, 576, 1536], P('pipe'), may hold values from -6 to 6
- bwd_inputs: bfloat16 [8, 576, 1536], P('pipe'), may hold values from -6 to 6
- bwd_cotangent: bfloat16 [8, 576, 1536], P('pipe'), may hold values from -6 to 6
- fwd_lengths: int32 [8, 8], P('pipe'), may hold values from 1 to 192, 576 in all within a row
- bwd_lengths: int32 [8, 8], P('pipe'), may hold values from 1 to 192, 576 in all within a row
- norm_gains: bfloat16 [2, 8, 1536], P(None, 'pipe'), may hold values from 0.25 to 1.75
- query_weight: bfloat16 [2, 8, 1536, 1536], P(None, 'pipe', None, 'tensor'), may hold values from -1 to 1
- key_weight: bfloat16 [2, 8, 1536, 1536], P(None, 'pipe', None, 'tensor'), may hold values from -1 to 1
- value_weight: bfloat16 [2, 8, 1536, 1536], P(None, 'pipe', None, 'tensor'), may hold values from -0.15625 to 0.15625
- out_weight: bfloat16 [2, 8, 1536, 1536], P(None, 'pipe', 'tensor'), may hold values from -0.15625 to 0.15625
Outputs:
- next_inputs: bfloat16 [8, 576, 1536], P('pipe', 'tensor')
- next_cotangent: bfloat16 [8, 576, 1536], P('pipe', 'tensor')
- out_weight_grad: float32 [8, 1536, 1536], P('pipe', 'tensor')
The draws below stay inside these ranges and needn't reach their ends.
Inputs may be any that keep to these rules, and one draw needn't show every extreme that they name: `fwd_lengths`: each microbatch's mesh lengths sum to 576; the longest is exactly 192. `bwd_lengths`: each microbatch's mesh lengths sum to 576; the longest is exactly 192.
All inputs are finite; a program needn't handle non-finite values.
Results may differ from the reference program's by a relative error of at most 0.019.
Values may be sent and summed in bfloat16 or wider, within the bound.
A program may use at most 64 MiB of HBM per device.

```python
import math
import jax
import jax.numpy as jnp
import numpy as np
from jax import lax

D = 1536
HEADS = 12
HEAD_DIM = 128
ROWS = 576
DOCS = 8
MOST = 192
SECTIONS = 8
N_TENSOR = 4


def own_normal(key, salt):
    return jnp.clip(jax.random.normal(jax.random.fold_in(key, salt), (2, SECTIONS, D, HEADS * HEAD_DIM), jnp.float32), -5.0, 5.0)


def projection_draw(key, salt):
    own = own_normal(key, salt)
    result = own * D ** (-0.5)
    return jnp.clip(result, -1.0, 1.0).astype(jnp.bfloat16)


def draw_query_weight(key, part):
    return projection_draw(key, 202)


def draw_key_weight(key, part):
    return projection_draw(key, 303)


def shard_levels(stream_key, dims, pieces, low, largest):
    loudness, own = 1.0, jax.random.fold_in(stream_key, 6)
    for axis_at, blocks in pieces:
        heights = jnp.exp(jax.random.uniform(jax.random.fold_in(own, axis_at), (blocks,), jnp.float32, low / len(pieces), largest / len(pieces)))
        loudness = loudness * jnp.repeat(heights, dims[axis_at] // blocks).reshape([-1 if axis == axis_at else 1 for axis in range(len(dims))])
    return loudness


def profile(amount, total, bound, lean):
    weights = [(1 << 20) // math.isqrt(standing ** lean) + 1 for standing in range(2, amount + 1)]
    surplus, given = total - bound - (amount - 1), [1] * (amount - 1)
    while surplus > 0:
        free = [i for i in range(amount - 1) if given[i] < bound]
        whole, left = sum([weights[i] for i in free]), surplus
        for i in free:
            addition = min(bound - given[i], max(1, left * weights[i] // whole), surplus)
            given[i] = given[i] + addition
            surplus = surplus - addition
    return np.array([bound] + given)


def uneven(stream_key, amount, total, reach, lean):
    if amount == 2:
        one = jax.random.randint(stream_key, (), max(1, total - reach), min(reach, total - 1) + 1)
        return jnp.stack([one, total - one])
    tallies = jnp.asarray(profile(amount, total, reach, lean), jnp.int32)
    pairs = (amount - 1) // 2
    giver, sink = tallies[1:1 + 2 * pairs:2], tallies[2:2 + 2 * pairs:2]
    slack = jnp.minimum(giver - 1, reach - sink)
    shifted = jax.random.randint(jax.random.fold_in(stream_key, 1), (pairs,), 0, 1 << 20) % (slack + 1)
    tallies = tallies.at[1:1 + 2 * pairs:2].set(giver - shifted).at[2:2 + 2 * pairs:2].set(sink + shifted)
    return tallies[jax.random.permutation(jax.random.fold_in(stream_key, 2), amount)]


def normal_values(rng, extent, deviation, bound, pieces=(), kind=jnp.bfloat16):
    values = deviation * jax.random.normal(rng, extent, jnp.float32)
    if pieces:
        values = values * shard_levels(rng, extent, pieces, -0.22, 0.18)
    return jnp.clip(values, -bound, bound).astype(kind)


def setup_inputs(seed: int = 0) -> dict:
    key_of = jax.random.split(jax.random.key(seed), 11)
    return {
        "fwd_inputs": normal_values(key_of[0], (SECTIONS, ROWS, D), 1.0, 6.0, ((0, 8),)),
        "bwd_inputs": normal_values(key_of[1], (SECTIONS, ROWS, D), 1.0, 6.0, ((0, 8),)),
        "bwd_cotangent": normal_values(key_of[2], (SECTIONS, ROWS, D), 1.0, 6.0, ((0, 8),)),
        "fwd_lengths": jax.vmap(lambda own: uneven(own, DOCS, ROWS, MOST, 2))(jax.random.split(key_of[3], SECTIONS)).reshape((SECTIONS, DOCS)).astype(jnp.int32),
        "bwd_lengths": jax.vmap(lambda own: uneven(own, DOCS, ROWS, MOST, 2))(jax.random.split(key_of[4], SECTIONS)).reshape((SECTIONS, DOCS)).astype(jnp.int32),
        "norm_gains": jnp.clip(1.0 + 0.15 * jax.random.normal(key_of[5], (2, SECTIONS, D), jnp.float32), 0.25, 1.75).astype(jnp.bfloat16),
        "query_weight": draw_query_weight(jax.random.fold_in(key_of[10], 71), 0),
        "key_weight": draw_key_weight(jax.random.fold_in(key_of[10], 71), 0),
        "value_weight": normal_values(key_of[8], (2, SECTIONS, D, HEADS * HEAD_DIM), D ** -0.5, 0.15625, ((1, 8), (3, 4))),
        "out_weight": normal_values(key_of[9], (2, SECTIONS, HEADS * HEAD_DIM, D), (HEADS * HEAD_DIM) ** -0.5, 0.15625, ((1, 8), (2, 4))),
    }


def rms_norm(activation, gain_vec):
    widened = activation.astype(jnp.float32)
    mean_square = lax.optimization_barrier(jnp.mean(widened * widened, axis=-1, keepdims=True))
    return (widened * lax.rsqrt(mean_square + 1e-05) * gain_vec.astype(jnp.float32)).astype(jnp.bfloat16)

def doc_mask(lengths, row_count):
    doc_ends = jnp.cumsum(lengths).astype(jnp.int32)
    position = jnp.arange(row_count, dtype=jnp.int32)
    segment = lax.optimization_barrier(jnp.sum((position[:, None] >= doc_ends[None, :]).astype(jnp.int32), axis=1))
    return (segment[:, None] == segment[None, :]) & (position[None, :] <= position[:, None])

def head_block(normed, w_query, w_key, w_value, w_out, keep_mask):
    row_count = normed.shape[0]
    group_count = w_query.shape[1] // HEAD_DIM

    def project(weight):
        return jnp.dot(normed, weight, preferred_element_type=jnp.float32).astype(jnp.bfloat16).reshape(row_count, group_count, HEAD_DIM)
    queries = project(w_query)
    key_rows = project(w_key)
    value_rows = project(w_value)
    scores = jnp.einsum('qgh,kgh->gqk', queries.astype(jnp.float32), key_rows.astype(jnp.float32)) * HEAD_DIM ** (-0.5)
    scores = jnp.where(keep_mask[None], scores, -1e+30)
    row_max = lax.optimization_barrier(jnp.max(scores, axis=-1, keepdims=True))
    weights = jnp.where(keep_mask[None], jnp.exp(scores - row_max), 0.0)
    weights_bf = (weights / lax.optimization_barrier(jnp.sum(weights, axis=-1, keepdims=True))).astype(jnp.bfloat16)
    attended = jnp.einsum('gqk,kgh->qgh', weights_bf.astype(jnp.float32), value_rows.astype(jnp.float32)).astype(jnp.bfloat16)
    attended = attended.reshape(row_count, group_count * HEAD_DIM)
    return (jnp.dot(attended, w_out, preferred_element_type=jnp.float32), attended)

def section_forward(inputs, gain_vec, w_query, w_key, w_value, w_out, lengths):
    keep_mask = doc_mask(lengths, inputs.shape[0])
    normed = rms_norm(inputs, gain_vec)
    group_width = w_query.shape[1] // N_TENSOR
    total = jnp.zeros(inputs.shape, jnp.float32)
    for member in range(N_TENSOR):
        column_span = slice(member * group_width, (member + 1) * group_width)
        partial_out, unused = head_block(normed, w_query[:, column_span], w_key[:, column_span], w_value[:, column_span], w_out[column_span, :], keep_mask)
        rounded = lax.optimization_barrier(partial_out.astype(jnp.bfloat16))
        total = total + rounded.astype(jnp.float32)
    return (inputs.astype(jnp.float32) + total).astype(jnp.bfloat16)

def section_backward(inputs, cotangent, gain_vec, w_query, w_key, w_value, w_out, lengths):
    keep_mask = doc_mask(lengths, inputs.shape[0])
    group_width = w_query.shape[1] // N_TENSOR
    total = jnp.zeros(inputs.shape, jnp.float32)
    grad_parts = []
    for member in range(N_TENSOR):
        column_span = slice(member * group_width, (member + 1) * group_width)

        def branch(activation):
            return head_block(rms_norm(activation, gain_vec), w_query[:, column_span], w_key[:, column_span], w_value[:, column_span], w_out[column_span, :], keep_mask)
        unused, pull_back, attended = jax.vjp(branch, inputs, has_aux=True)
        input_grad, = pull_back(cotangent.astype(jnp.float32))
        total = total + input_grad.astype(jnp.float32)
        grad_parts.append(lax.dot_general(attended, cotangent, (((0,), (0,)), ((), ())), preferred_element_type=jnp.float32))
    return ((cotangent.astype(jnp.float32) + total).astype(jnp.bfloat16), jnp.concatenate(grad_parts, axis=0))

def reference(fwd_inputs, bwd_inputs, bwd_cotangent, fwd_lengths, bwd_lengths, norm_gains, query_weight, key_weight, value_weight, out_weight):

    def per_section(bundle):
        fin, bin_, bcot, flen, blen, gain_f, gain_b, wq_f, wq_b, wk_f, wk_b, wv_f, wv_b, wo_f, wo_b = bundle
        section_out = section_forward(fin, gain_f, wq_f, wk_f, wv_f, wo_f, flen)
        input_cot, grad_mirror = section_backward(bin_, bcot, gain_b, wq_b, wk_b, wv_b, wo_b, blen)
        return (section_out, input_cot, grad_mirror)
    section_outs, input_cots, grad_mirrors = lax.map(per_section, (fwd_inputs, bwd_inputs, bwd_cotangent, fwd_lengths, bwd_lengths, norm_gains[0], norm_gains[1], query_weight[0], query_weight[1], key_weight[0], key_weight[1], value_weight[0], value_weight[1], out_weight[0], out_weight[1]))
    zero_block = jnp.zeros((1,) + section_outs.shape[1:], jnp.bfloat16)
    next_inputs = jnp.concatenate([zero_block, section_outs[:-1]], axis=0)
    next_cotangent = jnp.concatenate([zero_block, input_cots[:-1]], axis=0)
    out_weight_grad = jnp.flip(grad_mirrors, axis=0)
    return (next_inputs, next_cotangent, out_weight_grad)
```

```python
import jax
import jax.numpy as jnp
from jax import lax
from jax.sharding import PartitionSpec as P

HEAD_DIM = 128


def passed_along(value, axis, by):
    peers = lax.axis_size(axis)
    pairs = [(i, i + by) for i in range(peers) if 0 <= i + by < peers]
    return lax.ppermute(value, axis, pairs)


def mirror_exchange(value, axis):
    peers = lax.axis_size(axis)
    return lax.ppermute(value, axis, [(i, peers - 1 - i) for i in range(peers)])


def rms_norm(activation, gain_vec):
    widened = activation.astype(jnp.float32)
    mean_square = jnp.mean(widened * widened, axis=-1, keepdims=True)
    return (widened * lax.rsqrt(mean_square + 1e-05) * gain_vec.astype(jnp.float32)).astype(
        jnp.bfloat16
    )


def doc_mask(lengths, row_count):
    doc_ends = jnp.cumsum(lengths)
    position = jnp.arange(row_count, dtype=jnp.int32)
    segment = jnp.sum((position[:, None] >= doc_ends[None, :]).astype(jnp.int32), axis=1)
    return (segment[:, None] == segment[None, :]) & (position[None, :] <= position[:, None])


def head_block(normed, w_query, w_key, w_value, w_out, keep_mask):
    row_count = normed.shape[0]
    group_count = w_query.shape[1] // HEAD_DIM

    def project(weight):
        return (
            jnp.dot(normed, weight, preferred_element_type=jnp.float32)
            .astype(jnp.bfloat16)
            .reshape(row_count, group_count, HEAD_DIM)
        )

    queries = project(w_query)
    key_rows = project(w_key)
    value_rows = project(w_value)
    scores = jnp.einsum(
        "qgh,kgh->gqk", queries.astype(jnp.float32), key_rows.astype(jnp.float32)
    ) * HEAD_DIM ** (-0.5)
    scores = jnp.where(keep_mask[None], scores, -1e30)
    row_max = jnp.max(scores, axis=-1, keepdims=True)
    weights = jnp.where(keep_mask[None], jnp.exp(scores - row_max), 0.0)
    weights_bf = (weights / jnp.sum(weights, axis=-1, keepdims=True)).astype(jnp.bfloat16)
    attended = jnp.einsum(
        "gqk,kgh->qgh", weights_bf.astype(jnp.float32), value_rows.astype(jnp.float32)
    ).astype(jnp.bfloat16)
    attended = attended.reshape(row_count, group_count * HEAD_DIM)
    return (jnp.dot(attended, w_out, preferred_element_type=jnp.float32), attended)


def per_device(
    fwd_inputs,
    bwd_inputs,
    bwd_cotangent,
    fwd_lengths,
    bwd_lengths,
    norm_gains,
    query_weight,
    key_weight,
    value_weight,
    out_weight,
):
    row_count = fwd_inputs.shape[1]
    share_rows = row_count // lax.axis_size("tensor")
    row_start = lax.axis_index("tensor") * share_rows
    forward_in = fwd_inputs[0]
    forward_mask = doc_mask(fwd_lengths[0], row_count)
    forward_term, unused = head_block(
        rms_norm(forward_in, norm_gains[0, 0]),
        query_weight[0, 0],
        key_weight[0, 0],
        value_weight[0, 0],
        out_weight[0, 0],
        forward_mask,
    )
    backward_in = bwd_inputs[0]
    cotangent = bwd_cotangent[0]
    backward_mask = doc_mask(bwd_lengths[0], row_count)

    def branch(activation):
        return head_block(
            rms_norm(activation, norm_gains[1, 0]),
            query_weight[1, 0],
            key_weight[1, 0],
            value_weight[1, 0],
            out_weight[1, 0],
            backward_mask,
        )

    unused_out, pull_back, attended = jax.vjp(branch, backward_in, has_aux=True)
    (input_grad,) = pull_back(cotangent.astype(jnp.float32))
    weight_grad = lax.dot_general(
        attended, cotangent, (((0,), (0,)), ((), ())), preferred_element_type=jnp.float32
    )
    backward_term = input_grad.astype(jnp.float32)
    summed_forward = lax.psum_scatter(
        forward_term.astype(jnp.bfloat16), "tensor", scatter_dimension=0, tiled=True
    ).astype(jnp.float32)
    summed_backward = lax.psum_scatter(
        backward_term.astype(jnp.bfloat16), "tensor", scatter_dimension=0, tiled=True
    ).astype(jnp.float32)
    forward_rows = lax.dynamic_slice_in_dim(forward_in, row_start, share_rows, 0)
    cotangent_rows = lax.dynamic_slice_in_dim(cotangent, row_start, share_rows, 0)
    section_rows = (forward_rows.astype(jnp.float32) + summed_forward).astype(jnp.bfloat16)
    grad_rows = (cotangent_rows.astype(jnp.float32) + summed_backward).astype(jnp.bfloat16)
    moved_section = passed_along(section_rows, "pipe", 1)
    moved_grad = passed_along(grad_rows, "pipe", 1)
    mirrored = mirror_exchange(weight_grad.astype(jnp.bfloat16), "pipe").astype(jnp.float32)
    return (moved_section[None], moved_grad[None], mirrored[None])


def solution(mesh):
    placed = (
        P("pipe", None, None),
        P("pipe", None, None),
        P("pipe", None, None),
        P("pipe", None),
        P("pipe", None),
        P(None, "pipe", None),
        P(None, "pipe", None, "tensor"),
        P(None, "pipe", None, "tensor"),
        P(None, "pipe", None, "tensor"),
        P(None, "pipe", "tensor", None),
    )
    return jax.shard_map(
        per_device,
        mesh=mesh,
        in_specs=placed,
        out_specs=(P("pipe", "tensor", None), P("pipe", "tensor", None), P("pipe", "tensor", None)),
        check_vma=False,
    )
```

```python
import jax
import jax.numpy as jnp
from jax import lax
from jax.experimental import pallas as pl
from jax.experimental.pallas import tpu as pltpu
from jax.sharding import PartitionSpec as P

HEAD_DIM = 128
MOST = 192
VMEM_LIMIT = 48 * 1024 * 1024


def passed_along(value, axis, by):
    peers = lax.axis_size(axis)
    pairs = [(i, i + by) for i in range(peers) if 0 <= i + by < peers]
    return lax.ppermute(value, axis, pairs)


def mirror_exchange(value, axis):
    peers = lax.axis_size(axis)
    return lax.ppermute(value, axis, [(i, peers - 1 - i) for i in range(peers)])


def doc_start(lengths_ref, first_row, row_count):
    position = lax.broadcasted_iota(jnp.int32, (row_count, 1), 0) + first_row
    start = jnp.zeros((row_count, 1), jnp.int32)
    end = jnp.int32(0)
    for doc in range(lengths_ref.shape[1]):
        end = end + lengths_ref[0, doc]
        start = jnp.where(position >= end, end, start)
    return position, start


def dot_nn(left, right):
    return jnp.dot(left, right, preferred_element_type=jnp.float32)


def dot_nt(left, right):
    return lax.dot_general(
        left, right, (((1,), (1,)), ((), ())), preferred_element_type=jnp.float32
    )


def dot_tn(left, right):
    return lax.dot_general(
        left, right, (((0,), (0,)), ((), ())), preferred_element_type=jnp.float32
    )


def start_copies(pairs, sems):
    copies = []
    for index, (source, target) in enumerate(pairs):
        copy = pltpu.make_async_copy(source, target, sems.at[index])
        copy.start()
        copies.append(copy)
    return copies


def normed_rows(x_ref, gain, rows):
    widened = x_ref[rows, :].astype(jnp.float32)
    mean_square = jnp.mean(widened * widened, axis=-1, keepdims=True)
    scale = lax.rsqrt(mean_square + 1e-05)
    return (widened * scale * gain).astype(jnp.bfloat16), scale


def score_block(queries, key_rows, keep):
    scores = dot_nt(queries, key_rows) * HEAD_DIM ** (-0.5)
    scores = jnp.where(keep, scores, -1e30)
    weights = jnp.exp(scores - jnp.max(scores, axis=-1, keepdims=True))
    return weights, 1.0 / jnp.sum(weights, axis=-1, keepdims=True)


def window_mask(lengths_ref, first_row, first_key, last_key):
    position, start = doc_start(lengths_ref, first_row, MOST)
    keys = lax.broadcasted_iota(jnp.int32, (MOST, last_key - first_key), 1) + first_key
    return (keys >= start) & (keys <= position)


def forward_kernel(
    lengths_ref, gain_ref, x_hbm, wq_hbm, wk_hbm, wv_hbm, wo_hbm, out_ref,
    x_ref, w_ref, wo_ref, qkv_ref, sems,
):
    width = wq_hbm.shape[3]
    copies = start_copies(
        [
            (x_hbm.at[0], x_ref),
            (wq_hbm.at[0, 0], w_ref.at[:, 0:width]),
            (wk_hbm.at[0, 0], w_ref.at[:, width : 2 * width]),
            (wv_hbm.at[0, 0], w_ref.at[:, 2 * width : 3 * width]),
            (wo_hbm.at[0, 0], wo_ref),
        ],
        sems,
    )
    gain = gain_ref[0].astype(jnp.float32)
    copies[0].wait()
    blocks = x_ref.shape[0] // MOST
    for block in range(blocks):
        low, high = block * MOST, (block + 1) * MOST
        normed, unused = normed_rows(x_ref, gain, slice(low, high))
        if block == 0:
            for copy in copies[1:4]:
                copy.wait()
        qkv_ref[low:high, :] = dot_nn(normed, w_ref[...]).astype(jnp.bfloat16)
    for block in range(blocks):
        low, high = block * MOST, (block + 1) * MOST
        key_low = max(0, low - MOST)
        keep = window_mask(lengths_ref, low, key_low, high)
        parts = []
        for head in range(width // HEAD_DIM):
            at = head * HEAD_DIM
            weights, inverse = score_block(
                qkv_ref[low:high, at : at + HEAD_DIM],
                qkv_ref[key_low:high, width + at : width + at + HEAD_DIM],
                keep,
            )
            mixed = dot_nn(
                (weights * inverse).astype(jnp.bfloat16),
                qkv_ref[key_low:high, 2 * width + at : 2 * width + at + HEAD_DIM],
            )
            parts.append(mixed.astype(jnp.bfloat16))
        attended = jnp.concatenate(parts, axis=1)
        if block == 0:
            copies[4].wait()
        out_ref[low:high, :] = dot_nn(attended, wo_ref[...]).astype(jnp.bfloat16)


def backward_kernel(
    lengths_ref, gain_ref, x_hbm, c_hbm, wq_hbm, wk_hbm, wv_hbm, wo_hbm, out_ref, grad_ref,
    x_ref, c_ref, w_ref, wo_ref, qkv_ref, dqkv_ref, att_ref, sems,
):
    width = wq_hbm.shape[3]
    copies = start_copies(
        [
            (x_hbm.at[0], x_ref),
            (wq_hbm.at[1, 0], w_ref.at[:, 0:width]),
            (wk_hbm.at[1, 0], w_ref.at[:, width : 2 * width]),
            (wv_hbm.at[1, 0], w_ref.at[:, 2 * width : 3 * width]),
            (c_hbm.at[0], c_ref),
            (wo_hbm.at[1, 0], wo_ref),
        ],
        sems,
    )
    gain = gain_ref[1].astype(jnp.float32)
    copies[0].wait()
    blocks = x_ref.shape[0] // MOST
    heads = width // HEAD_DIM
    scales = []
    for block in range(blocks):
        low, high = block * MOST, (block + 1) * MOST
        normed, scale = normed_rows(x_ref, gain, slice(low, high))
        scales.append(scale)
        if block == 0:
            for copy in copies[1:4]:
                copy.wait()
        qkv_ref[low:high, :] = dot_nn(normed, w_ref[...]).astype(jnp.bfloat16)
    copies[4].wait()
    copies[5].wait()
    carried = {}
    for block in range(blocks):
        low, high = block * MOST, (block + 1) * MOST
        key_low = max(0, low - MOST)
        keep = window_mask(lengths_ref, low, key_low, high)
        d_attended = dot_nt(c_ref[low:high, :], wo_ref[...]).astype(jnp.bfloat16)
        for head in range(heads):
            at = head * HEAD_DIM
            cols = [slice(part * width + at, part * width + at + HEAD_DIM) for part in range(3)]
            queries = qkv_ref[low:high, cols[0]]
            key_rows = qkv_ref[key_low:high, cols[1]]
            value_rows = qkv_ref[key_low:high, cols[2]]
            weights, inverse = score_block(queries, key_rows, keep)
            probs = weights * inverse
            probs_bf = probs.astype(jnp.bfloat16)
            mixed = dot_nn(probs_bf, value_rows)
            att_ref[low:high, at : at + HEAD_DIM] = mixed.astype(jnp.bfloat16)
            d_mixed = d_attended[:, at : at + HEAD_DIM]
            d_probs = dot_nt(d_mixed, value_rows)
            delta = jnp.sum(mixed * d_mixed.astype(jnp.float32), axis=-1, keepdims=True)
            d_scores = (probs * (d_probs - delta) * HEAD_DIM ** (-0.5)).astype(jnp.bfloat16)
            dqkv_ref[low:high, cols[0]] = dot_nn(d_scores, key_rows).astype(jnp.bfloat16)
            d_keys = dot_tn(d_scores, queries)
            d_values = dot_tn(probs_bf, d_mixed)
            if block > 0:
                past_keys, past_values = carried[head]
                dqkv_ref[key_low:low, cols[1]] = (past_keys + d_keys[:MOST]).astype(jnp.bfloat16)
                dqkv_ref[key_low:low, cols[2]] = (past_values + d_values[:MOST]).astype(
                    jnp.bfloat16
                )
                d_keys, d_values = d_keys[MOST:], d_values[MOST:]
            if block == blocks - 1:
                dqkv_ref[low:high, cols[1]] = d_keys.astype(jnp.bfloat16)
                dqkv_ref[low:high, cols[2]] = d_values.astype(jnp.bfloat16)
            carried[head] = (d_keys, d_values)
    for block in range(blocks):
        low, high = block * MOST, (block + 1) * MOST
        d_normed = dot_nt(dqkv_ref[low:high, :], w_ref[...]) * gain
        widened = x_ref[low:high, :].astype(jnp.float32)
        scale = scales[block]
        pull = jnp.mean(d_normed * widened, axis=-1, keepdims=True) * scale * scale * scale
        out_ref[low:high, :] = (d_normed * scale - widened * pull).astype(jnp.bfloat16)
    for head in range(heads):
        at = head * HEAD_DIM
        grad_ref[at : at + HEAD_DIM, :] = dot_tn(
            att_ref[:, at : at + HEAD_DIM], c_ref[...]
        ).astype(jnp.bfloat16)


SMEM_SPEC = pl.BlockSpec(memory_space=pltpu.SMEM)
VMEM_SPEC = pl.BlockSpec(memory_space=pltpu.VMEM)
ANY_SPEC = pl.BlockSpec(memory_space=pl.ANY)


def forward_term_of(lengths, gains, x, wq, wk, wv, wo):
    rows, wide, width = x.shape[1], x.shape[2], wq.shape[3]
    bf16 = jnp.bfloat16
    return pl.pallas_call(
        forward_kernel,
        out_shape=jax.ShapeDtypeStruct((rows, wide), bf16),
        in_specs=[SMEM_SPEC, VMEM_SPEC] + [ANY_SPEC] * 5,
        out_specs=VMEM_SPEC,
        scratch_shapes=[
            pltpu.VMEM((rows, wide), bf16),
            pltpu.VMEM((wide, 3 * width), bf16),
            pltpu.VMEM((width, wide), bf16),
            pltpu.VMEM((rows, 3 * width), bf16),
            pltpu.SemaphoreType.DMA((5,)),
        ],
        compiler_params=pltpu.CompilerParams(vmem_limit_bytes=VMEM_LIMIT),
        cost_estimate=pl.CostEstimate(
            flops=8 * rows * wide * width, bytes_accessed=8 * wide * (rows + width),
            transcendentals=rows * MOST,
        ),
        name="forward_section",
    )(lengths, gains, x, wq, wk, wv, wo)


def backward_terms_of(lengths, gains, x, c, wq, wk, wv, wo):
    rows, wide, width = x.shape[1], x.shape[2], wq.shape[3]
    bf16 = jnp.bfloat16
    return pl.pallas_call(
        backward_kernel,
        out_shape=(
            jax.ShapeDtypeStruct((rows, wide), bf16),
            jax.ShapeDtypeStruct((width, wide), bf16),
        ),
        in_specs=[SMEM_SPEC, VMEM_SPEC] + [ANY_SPEC] * 6,
        out_specs=(VMEM_SPEC, VMEM_SPEC),
        scratch_shapes=[
            pltpu.VMEM((rows, wide), bf16),
            pltpu.VMEM((rows, wide), bf16),
            pltpu.VMEM((wide, 3 * width), bf16),
            pltpu.VMEM((width, wide), bf16),
            pltpu.VMEM((rows, 3 * width), bf16),
            pltpu.VMEM((rows, 3 * width), bf16),
            pltpu.VMEM((rows, width), bf16),
            pltpu.SemaphoreType.DMA((6,)),
        ],
        compiler_params=pltpu.CompilerParams(vmem_limit_bytes=VMEM_LIMIT),
        cost_estimate=pl.CostEstimate(
            flops=16 * rows * wide * width, bytes_accessed=8 * wide * (rows + width),
            transcendentals=rows * MOST,
        ),
        name="backward_section",
    )(lengths, gains, x, c, wq, wk, wv, wo)


def per_device(
    fwd_inputs,
    bwd_inputs,
    bwd_cotangent,
    fwd_lengths,
    bwd_lengths,
    norm_gains,
    query_weight,
    key_weight,
    value_weight,
    out_weight,
):
    row_count = fwd_inputs.shape[1]
    share_rows = row_count // lax.axis_size("tensor")
    row_start = lax.axis_index("tensor") * share_rows
    forward_in = fwd_inputs[0]
    cotangent = bwd_cotangent[0]
    forward_term = forward_term_of(
        fwd_lengths, norm_gains, fwd_inputs, query_weight, key_weight, value_weight, out_weight
    )
    backward_term, weight_grad = backward_terms_of(
        bwd_lengths,
        norm_gains,
        bwd_inputs,
        bwd_cotangent,
        query_weight,
        key_weight,
        value_weight,
        out_weight,
    )
    summed_forward = lax.psum_scatter(
        forward_term, "tensor", scatter_dimension=0, tiled=True
    ).astype(jnp.float32)
    summed_backward = lax.psum_scatter(
        backward_term, "tensor", scatter_dimension=0, tiled=True
    ).astype(jnp.float32)
    forward_rows = lax.dynamic_slice_in_dim(forward_in, row_start, share_rows, 0)
    cotangent_rows = lax.dynamic_slice_in_dim(cotangent, row_start, share_rows, 0)
    section_rows = (forward_rows.astype(jnp.float32) + summed_forward).astype(jnp.bfloat16)
    grad_rows = (cotangent_rows.astype(jnp.float32) + summed_backward).astype(jnp.bfloat16)
    moved_section = passed_along(section_rows, "pipe", 1)
    moved_grad = passed_along(grad_rows, "pipe", 1)
    mirrored = mirror_exchange(weight_grad, "pipe").astype(jnp.float32)
    return (moved_section[None], moved_grad[None], mirrored[None])


def solution(mesh):
    placed = (
        P("pipe", None, None),
        P("pipe", None, None),
        P("pipe", None, None),
        P("pipe", None),
        P("pipe", None),
        P(None, "pipe", None),
        P(None, "pipe", None, "tensor"),
        P(None, "pipe", None, "tensor"),
        P(None, "pipe", None, "tensor"),
        P(None, "pipe", "tensor", None),
    )
    return jax.shard_map(
        per_device,
        mesh=mesh,
        in_specs=placed,
        out_specs=(P("pipe", "tensor", None), P("pipe", "tensor", None), P("pipe", "tensor", None)),
        check_vma=False,
    )
```

```python
import jax
import jax.numpy as jnp
from jax import lax
from jax.experimental import pallas as pl
from jax.experimental.pallas import tpu as pltpu
from jax.sharding import PartitionSpec as P

HEAD_DIM = 128
MOST = 192
VMEM_LIMIT = 48 * 1024 * 1024


def passed_along(value, axis, by):
    peers = lax.axis_size(axis)
    pairs = [(i, i + by) for i in range(peers) if 0 <= i + by < peers]
    return lax.ppermute(value, axis, pairs)


def chain_sums_along(term, own_rows, axis, along):
    peers = lax.axis_size(axis)
    here = lax.axis_index(axis)
    share = term.shape[0] // peers

    def rows_of(owner):
        owner = jnp.clip(owner, 0, peers - 1)
        return lax.dynamic_slice_in_dim(term, owner * share, share, 0).astype(jnp.float32)

    own = passed_along((own_rows.astype(jnp.float32) + rows_of(here)).astype(jnp.bfloat16), along, 1)
    from_left = jnp.zeros((share, term.shape[1]), jnp.bfloat16)
    from_right = from_left
    for step in range(1, peers):
        going_right = (rows_of(peers - step + here) + from_left.astype(jnp.float32)).astype(
            jnp.bfloat16
        )
        going_left = (rows_of(here + step - peers) + from_right.astype(jnp.float32)).astype(
            jnp.bfloat16
        )
        right = [(i, i + 1) for i in range(step)]
        left = [(peers - 1 - i, peers - 2 - i) for i in range(step)]
        names = axis
        if step == peers - 1:
            names = (along, axis)
            right, left = (
                [
                    (stage * peers + source, (stage + 1) * peers + target)
                    for stage in range(lax.axis_size(along) - 1)
                    for source, target in pairs
                ]
                for pairs in (right, left)
            )
        from_left = lax.ppermute(going_right, names, right)
        from_right = lax.ppermute(going_left, names, left)
    total = own.astype(jnp.float32) + from_left.astype(jnp.float32)
    return (total + from_right.astype(jnp.float32)).astype(jnp.bfloat16)


def mirror_exchange(value, axis):
    peers = lax.axis_size(axis)
    return lax.ppermute(value, axis, [(i, peers - 1 - i) for i in range(peers)])


def doc_start(lengths_ref, first_row, row_count):
    position = lax.broadcasted_iota(jnp.int32, (row_count, 1), 0) + first_row
    start = jnp.zeros((row_count, 1), jnp.int32)
    end = jnp.int32(0)
    for doc in range(lengths_ref.shape[1]):
        end = end + lengths_ref[0, doc]
        start = jnp.where(position >= end, end, start)
    return position, start


def dot_nn(left, right):
    return jnp.dot(left, right, preferred_element_type=jnp.float32)


def dot_nt(left, right):
    return lax.dot_general(
        left, right, (((1,), (1,)), ((), ())), preferred_element_type=jnp.float32
    )


def dot_tn(left, right):
    return lax.dot_general(
        left, right, (((0,), (0,)), ((), ())), preferred_element_type=jnp.float32
    )


def start_copies(pairs, sems):
    copies = []
    for index, (source, target) in enumerate(pairs):
        copy = pltpu.make_async_copy(source, target, sems.at[index])
        copy.start()
        copies.append(copy)
    return copies


def normed_rows(x_ref, gain, rows):
    widened = x_ref[rows, :].astype(jnp.float32)
    mean_square = jnp.mean(widened * widened, axis=-1, keepdims=True)
    scale = lax.rsqrt(mean_square + 1e-05)
    return (widened * scale * gain).astype(jnp.bfloat16), scale


def score_block(queries, key_rows, keep):
    scores = dot_nt(queries, key_rows) * HEAD_DIM ** (-0.5)
    scores = jnp.where(keep, scores, -1e30)
    weights = jnp.exp(scores - jnp.max(scores, axis=-1, keepdims=True))
    return weights, 1.0 / jnp.sum(weights, axis=-1, keepdims=True)


def window_mask(lengths_ref, first_row, first_key, last_key):
    position, start = doc_start(lengths_ref, first_row, MOST)
    keys = lax.broadcasted_iota(jnp.int32, (MOST, last_key - first_key), 1) + first_key
    return (keys >= start) & (keys <= position)


def forward_kernel(
    lengths_ref, gain_ref, x_hbm, wq_hbm, wk_hbm, wv_hbm, wo_hbm, out_ref,
    x_ref, w_ref, wo_ref, qkv_ref, sems,
):
    width = wq_hbm.shape[3]
    copies = start_copies(
        [
            (x_hbm.at[0], x_ref),
            (wq_hbm.at[0, 0], w_ref.at[:, 0:width]),
            (wk_hbm.at[0, 0], w_ref.at[:, width : 2 * width]),
            (wv_hbm.at[0, 0], w_ref.at[:, 2 * width : 3 * width]),
            (wo_hbm.at[0, 0], wo_ref),
        ],
        sems,
    )
    gain = gain_ref[0].astype(jnp.float32)
    copies[0].wait()
    blocks = x_ref.shape[0] // MOST
    for block in range(blocks):
        low, high = block * MOST, (block + 1) * MOST
        normed, unused = normed_rows(x_ref, gain, slice(low, high))
        if block == 0:
            for copy in copies[1:4]:
                copy.wait()
        qkv_ref[low:high, :] = dot_nn(normed, w_ref[...]).astype(jnp.bfloat16)
    for block in range(blocks):
        low, high = block * MOST, (block + 1) * MOST
        key_low = max(0, low - MOST)
        keep = window_mask(lengths_ref, low, key_low, high)
        parts = []
        for head in range(width // HEAD_DIM):
            at = head * HEAD_DIM
            weights, inverse = score_block(
                qkv_ref[low:high, at : at + HEAD_DIM],
                qkv_ref[key_low:high, width + at : width + at + HEAD_DIM],
                keep,
            )
            mixed = dot_nn(
                (weights * inverse).astype(jnp.bfloat16),
                qkv_ref[key_low:high, 2 * width + at : 2 * width + at + HEAD_DIM],
            )
            parts.append(mixed.astype(jnp.bfloat16))
        attended = jnp.concatenate(parts, axis=1)
        if block == 0:
            copies[4].wait()
        out_ref[low:high, :] = dot_nn(attended, wo_ref[...]).astype(jnp.bfloat16)


def backward_kernel(
    lengths_ref, gain_ref, x_hbm, c_hbm, wq_hbm, wk_hbm, wv_hbm, wo_hbm, out_ref, grad_ref,
    x_ref, c_ref, w_ref, wo_ref, qkv_ref, dqkv_ref, att_ref, sems,
):
    width = wq_hbm.shape[3]
    copies = start_copies(
        [
            (x_hbm.at[0], x_ref),
            (wq_hbm.at[1, 0], w_ref.at[:, 0:width]),
            (wk_hbm.at[1, 0], w_ref.at[:, width : 2 * width]),
            (wv_hbm.at[1, 0], w_ref.at[:, 2 * width : 3 * width]),
            (c_hbm.at[0], c_ref),
            (wo_hbm.at[1, 0], wo_ref),
        ],
        sems,
    )
    gain = gain_ref[1].astype(jnp.float32)
    copies[0].wait()
    blocks = x_ref.shape[0] // MOST
    heads = width // HEAD_DIM
    scales = []
    for block in range(blocks):
        low, high = block * MOST, (block + 1) * MOST
        normed, scale = normed_rows(x_ref, gain, slice(low, high))
        scales.append(scale)
        if block == 0:
            for copy in copies[1:4]:
                copy.wait()
        qkv_ref[low:high, :] = dot_nn(normed, w_ref[...]).astype(jnp.bfloat16)
    copies[4].wait()
    copies[5].wait()
    carried = {}
    for block in range(blocks):
        low, high = block * MOST, (block + 1) * MOST
        key_low = max(0, low - MOST)
        keep = window_mask(lengths_ref, low, key_low, high)
        d_attended = dot_nt(c_ref[low:high, :], wo_ref[...]).astype(jnp.bfloat16)
        for head in range(heads):
            at = head * HEAD_DIM
            cols = [slice(part * width + at, part * width + at + HEAD_DIM) for part in range(3)]
            queries = qkv_ref[low:high, cols[0]]
            key_rows = qkv_ref[key_low:high, cols[1]]
            value_rows = qkv_ref[key_low:high, cols[2]]
            weights, inverse = score_block(queries, key_rows, keep)
            probs = weights * inverse
            probs_bf = probs.astype(jnp.bfloat16)
            mixed = dot_nn(probs_bf, value_rows)
            att_ref[low:high, at : at + HEAD_DIM] = mixed.astype(jnp.bfloat16)
            d_mixed = d_attended[:, at : at + HEAD_DIM]
            d_probs = dot_nt(d_mixed, value_rows)
            delta = jnp.sum(mixed * d_mixed.astype(jnp.float32), axis=-1, keepdims=True)
            d_scores = (probs * (d_probs - delta) * HEAD_DIM ** (-0.5)).astype(jnp.bfloat16)
            dqkv_ref[low:high, cols[0]] = dot_nn(d_scores, key_rows).astype(jnp.bfloat16)
            d_keys = dot_tn(d_scores, queries)
            d_values = dot_tn(probs_bf, d_mixed)
            if block > 0:
                past_keys, past_values = carried[head]
                dqkv_ref[key_low:low, cols[1]] = (past_keys + d_keys[:MOST]).astype(jnp.bfloat16)
                dqkv_ref[key_low:low, cols[2]] = (past_values + d_values[:MOST]).astype(
                    jnp.bfloat16
                )
                d_keys, d_values = d_keys[MOST:], d_values[MOST:]
            if block == blocks - 1:
                dqkv_ref[low:high, cols[1]] = d_keys.astype(jnp.bfloat16)
                dqkv_ref[low:high, cols[2]] = d_values.astype(jnp.bfloat16)
            carried[head] = (d_keys, d_values)
    for block in range(blocks):
        low, high = block * MOST, (block + 1) * MOST
        d_normed = dot_nt(dqkv_ref[low:high, :], w_ref[...]) * gain
        widened = x_ref[low:high, :].astype(jnp.float32)
        scale = scales[block]
        pull = jnp.mean(d_normed * widened, axis=-1, keepdims=True) * scale * scale * scale
        out_ref[low:high, :] = (d_normed * scale - widened * pull).astype(jnp.bfloat16)
    for head in range(heads):
        at = head * HEAD_DIM
        grad_ref[at : at + HEAD_DIM, :] = dot_tn(
            att_ref[:, at : at + HEAD_DIM], c_ref[...]
        ).astype(jnp.bfloat16)


SMEM_SPEC = pl.BlockSpec(memory_space=pltpu.SMEM)
VMEM_SPEC = pl.BlockSpec(memory_space=pltpu.VMEM)
ANY_SPEC = pl.BlockSpec(memory_space=pl.ANY)


def forward_term_of(lengths, gains, x, wq, wk, wv, wo):
    rows, wide, width = x.shape[1], x.shape[2], wq.shape[3]
    bf16 = jnp.bfloat16
    return pl.pallas_call(
        forward_kernel,
        out_shape=jax.ShapeDtypeStruct((rows, wide), bf16),
        in_specs=[SMEM_SPEC, VMEM_SPEC] + [ANY_SPEC] * 5,
        out_specs=VMEM_SPEC,
        scratch_shapes=[
            pltpu.VMEM((rows, wide), bf16),
            pltpu.VMEM((wide, 3 * width), bf16),
            pltpu.VMEM((width, wide), bf16),
            pltpu.VMEM((rows, 3 * width), bf16),
            pltpu.SemaphoreType.DMA((5,)),
        ],
        compiler_params=pltpu.CompilerParams(vmem_limit_bytes=VMEM_LIMIT),
        cost_estimate=pl.CostEstimate(
            flops=8 * rows * wide * width, bytes_accessed=8 * wide * (rows + width),
            transcendentals=rows * MOST,
        ),
        name="forward_section",
    )(lengths, gains, x, wq, wk, wv, wo)


def backward_terms_of(lengths, gains, x, c, wq, wk, wv, wo):
    rows, wide, width = x.shape[1], x.shape[2], wq.shape[3]
    bf16 = jnp.bfloat16
    return pl.pallas_call(
        backward_kernel,
        out_shape=(
            jax.ShapeDtypeStruct((rows, wide), bf16),
            jax.ShapeDtypeStruct((width, wide), bf16),
        ),
        in_specs=[SMEM_SPEC, VMEM_SPEC] + [ANY_SPEC] * 6,
        out_specs=(VMEM_SPEC, VMEM_SPEC),
        scratch_shapes=[
            pltpu.VMEM((rows, wide), bf16),
            pltpu.VMEM((rows, wide), bf16),
            pltpu.VMEM((wide, 3 * width), bf16),
            pltpu.VMEM((width, wide), bf16),
            pltpu.VMEM((rows, 3 * width), bf16),
            pltpu.VMEM((rows, 3 * width), bf16),
            pltpu.VMEM((rows, width), bf16),
            pltpu.SemaphoreType.DMA((6,)),
        ],
        compiler_params=pltpu.CompilerParams(vmem_limit_bytes=VMEM_LIMIT),
        cost_estimate=pl.CostEstimate(
            flops=16 * rows * wide * width, bytes_accessed=8 * wide * (rows + width),
            transcendentals=rows * MOST,
        ),
        name="backward_section",
    )(lengths, gains, x, c, wq, wk, wv, wo)


def per_device(
    fwd_inputs,
    bwd_inputs,
    bwd_cotangent,
    fwd_lengths,
    bwd_lengths,
    norm_gains,
    query_weight,
    key_weight,
    value_weight,
    out_weight,
):
    row_count = fwd_inputs.shape[1]
    share_rows = row_count // lax.axis_size("tensor")
    row_start = lax.axis_index("tensor") * share_rows
    forward_in = fwd_inputs[0]
    cotangent = bwd_cotangent[0]
    forward_term = forward_term_of(
        fwd_lengths, norm_gains, fwd_inputs, query_weight, key_weight, value_weight, out_weight
    )
    backward_term, weight_grad = backward_terms_of(
        bwd_lengths,
        norm_gains,
        bwd_inputs,
        bwd_cotangent,
        query_weight,
        key_weight,
        value_weight,
        out_weight,
    )
    forward_rows = lax.dynamic_slice_in_dim(forward_in, row_start, share_rows, 0)
    cotangent_rows = lax.dynamic_slice_in_dim(cotangent, row_start, share_rows, 0)
    moved_section = chain_sums_along(forward_term, forward_rows, "tensor", "pipe")
    moved_grad = chain_sums_along(backward_term, cotangent_rows, "tensor", "pipe")
    mirrored = mirror_exchange(weight_grad, "pipe").astype(jnp.float32)
    return (moved_section[None], moved_grad[None], mirrored[None])


def solution(mesh):
    placed = (
        P("pipe", None, None),
        P("pipe", None, None),
        P("pipe", None, None),
        P("pipe", None),
        P("pipe", None),
        P(None, "pipe", None),
        P(None, "pipe", None, "tensor"),
        P(None, "pipe", None, "tensor"),
        P(None, "pipe", None, "tensor"),
        P(None, "pipe", "tensor", None),
    )
    return jax.shard_map(
        per_device,
        mesh=mesh,
        in_specs=placed,
        out_specs=(P("pipe", "tensor", None), P("pipe", "tensor", None), P("pipe", "tensor", None)),
        check_vma=False,
    )
```

```python
import jax
import jax.numpy as jnp
from jax import lax
from jax.experimental import pallas as pl
from jax.experimental.pallas import tpu as pltpu
from jax.sharding import PartitionSpec as P

HEAD_DIM = 128
MOST = 192
VMEM_LIMIT = 48 * 1024 * 1024


def passed_along(value, axis, by):
    peers = lax.axis_size(axis)
    pairs = [(i, i + by) for i in range(peers) if 0 <= i + by < peers]
    return lax.ppermute(value, axis, pairs)


def chain_sums_along(term, own_rows, axis, along):
    peers = lax.axis_size(axis)
    here = lax.axis_index(axis)
    share = term.shape[0] // peers

    def rows_of(owner):
        owner = jnp.clip(owner, 0, peers - 1)
        return lax.dynamic_slice_in_dim(term, owner * share, share, 0).astype(jnp.float32)

    own = passed_along((own_rows.astype(jnp.float32) + rows_of(here)).astype(jnp.bfloat16), along, 1)
    from_left = jnp.zeros((share, term.shape[1]), jnp.bfloat16)
    from_right = from_left
    for step in range(1, peers):
        going_right = (rows_of(peers - step + here) + from_left.astype(jnp.float32)).astype(
            jnp.bfloat16
        )
        going_left = (rows_of(here + step - peers) + from_right.astype(jnp.float32)).astype(
            jnp.bfloat16
        )
        right = [(i, i + 1) for i in range(step)]
        left = [(peers - 1 - i, peers - 2 - i) for i in range(step)]
        names = axis
        if step == peers - 1:
            names = (along, axis)
            right, left = (
                [
                    (stage * peers + source, (stage + 1) * peers + target)
                    for stage in range(lax.axis_size(along) - 1)
                    for source, target in pairs
                ]
                for pairs in (right, left)
            )
        from_left = lax.ppermute(going_right, names, right)
        from_right = lax.ppermute(going_left, names, left)
    total = own.astype(jnp.float32) + from_left.astype(jnp.float32)
    return (total + from_right.astype(jnp.float32)).astype(jnp.bfloat16)


def mirror_exchange(value, axis):
    peers = lax.axis_size(axis)
    return lax.ppermute(value, axis, [(i, peers - 1 - i) for i in range(peers)])


def doc_start(lengths_ref, first_row, row_count):
    position = lax.broadcasted_iota(jnp.int32, (row_count, 1), 0) + first_row
    start = jnp.zeros((row_count, 1), jnp.int32)
    end = jnp.int32(0)
    for doc in range(lengths_ref.shape[1]):
        end = end + lengths_ref[0, doc]
        start = jnp.where(position >= end, end, start)
    return position, start


def dot_nn(left, right):
    return jnp.dot(left, right, preferred_element_type=jnp.float32)


def dot_nt(left, right):
    return lax.dot_general(
        left, right, (((1,), (1,)), ((), ())), preferred_element_type=jnp.float32
    )


def dot_tn(left, right):
    return lax.dot_general(
        left, right, (((0,), (0,)), ((), ())), preferred_element_type=jnp.float32
    )


def start_copies(pairs, sems):
    copies = []
    for index, (source, target) in enumerate(pairs):
        copy = pltpu.make_async_copy(source, target, sems.at[index])
        copy.start()
        copies.append(copy)
    return copies


def normed_rows(x_ref, gain, rows):
    widened = x_ref[rows, :].astype(jnp.float32)
    mean_square = jnp.mean(widened * widened, axis=-1, keepdims=True)
    scale = lax.rsqrt(mean_square + 1e-05)
    return (widened * scale * gain).astype(jnp.bfloat16), scale


def score_block(queries, key_rows, keep):
    scores = dot_nt(queries, key_rows) * HEAD_DIM ** (-0.5)
    scores = jnp.where(keep, scores, -1e30)
    weights = jnp.exp(scores - jnp.max(scores, axis=-1, keepdims=True))
    return weights, 1.0 / jnp.sum(weights, axis=-1, keepdims=True)


def window_mask(lengths_ref, first_row, first_key, last_key):
    position, start = doc_start(lengths_ref, first_row, MOST)
    keys = lax.broadcasted_iota(jnp.int32, (MOST, last_key - first_key), 1) + first_key
    return (keys >= start) & (keys <= position)


def forward_kernel(
    lengths_ref, gain_ref, x_hbm, wq_hbm, wk_hbm, wv_hbm, wo_hbm, out_ref,
    x_ref, w_ref, wo_ref, qkv_ref, sems,
):
    width = wq_hbm.shape[3]
    copies = start_copies(
        [
            (x_hbm.at[0], x_ref),
            (wq_hbm.at[0, 0], w_ref.at[:, 0:width]),
            (wk_hbm.at[0, 0], w_ref.at[:, width : 2 * width]),
            (wv_hbm.at[0, 0], w_ref.at[:, 2 * width : 3 * width]),
            (wo_hbm.at[0, 0], wo_ref),
        ],
        sems,
    )
    gain = gain_ref[0].astype(jnp.float32)
    copies[0].wait()
    blocks = x_ref.shape[0] // MOST
    for block in range(blocks):
        low, high = block * MOST, (block + 1) * MOST
        normed, unused = normed_rows(x_ref, gain, slice(low, high))
        if block == 0:
            for copy in copies[1:4]:
                copy.wait()
        qkv_ref[low:high, :] = dot_nn(normed, w_ref[...]).astype(jnp.bfloat16)
    for block in range(blocks):
        low, high = block * MOST, (block + 1) * MOST
        key_low = max(0, low - MOST)
        keep = window_mask(lengths_ref, low, key_low, high)
        parts = []
        for head in range(width // HEAD_DIM):
            at = head * HEAD_DIM
            weights, inverse = score_block(
                qkv_ref[low:high, at : at + HEAD_DIM],
                qkv_ref[key_low:high, width + at : width + at + HEAD_DIM],
                keep,
            )
            mixed = dot_nn(
                (weights * inverse).astype(jnp.bfloat16),
                qkv_ref[key_low:high, 2 * width + at : 2 * width + at + HEAD_DIM],
            )
            parts.append(mixed.astype(jnp.bfloat16))
        attended = jnp.concatenate(parts, axis=1)
        if block == 0:
            copies[4].wait()
        out_ref[low:high, :] = dot_nn(attended, wo_ref[...]).astype(jnp.bfloat16)


def backward_kernel(
    lengths_ref, gain_ref, x_hbm, c_hbm, wq_hbm, wk_hbm, wv_hbm, wo_hbm, out_ref, att_ref,
    x_ref, c_ref, w_ref, wo_ref, qkv_ref, dqkv_ref, sems,
):
    width = wq_hbm.shape[3]
    copies = start_copies(
        [
            (x_hbm.at[0], x_ref),
            (wq_hbm.at[1, 0], w_ref.at[:, 0:width]),
            (wk_hbm.at[1, 0], w_ref.at[:, width : 2 * width]),
            (wv_hbm.at[1, 0], w_ref.at[:, 2 * width : 3 * width]),
            (c_hbm.at[0], c_ref),
            (wo_hbm.at[1, 0], wo_ref),
        ],
        sems,
    )
    gain = gain_ref[1].astype(jnp.float32)
    copies[0].wait()
    blocks = x_ref.shape[0] // MOST
    heads = width // HEAD_DIM
    scales = []
    for block in range(blocks):
        low, high = block * MOST, (block + 1) * MOST
        normed, scale = normed_rows(x_ref, gain, slice(low, high))
        scales.append(scale)
        if block == 0:
            for copy in copies[1:4]:
                copy.wait()
        qkv_ref[low:high, :] = dot_nn(normed, w_ref[...]).astype(jnp.bfloat16)
    copies[4].wait()
    copies[5].wait()
    carried = {}
    for block in range(blocks):
        low, high = block * MOST, (block + 1) * MOST
        key_low = max(0, low - MOST)
        keep = window_mask(lengths_ref, low, key_low, high)
        d_attended = dot_nt(c_ref[low:high, :], wo_ref[...]).astype(jnp.bfloat16)
        for head in range(heads):
            at = head * HEAD_DIM
            cols = [slice(part * width + at, part * width + at + HEAD_DIM) for part in range(3)]
            queries = qkv_ref[low:high, cols[0]]
            key_rows = qkv_ref[key_low:high, cols[1]]
            value_rows = qkv_ref[key_low:high, cols[2]]
            weights, inverse = score_block(queries, key_rows, keep)
            probs = weights * inverse
            probs_bf = probs.astype(jnp.bfloat16)
            mixed = dot_nn(probs_bf, value_rows)
            att_ref[low:high, at : at + HEAD_DIM] = mixed.astype(jnp.bfloat16)
            d_mixed = d_attended[:, at : at + HEAD_DIM]
            d_probs = dot_nt(d_mixed, value_rows)
            delta = jnp.sum(mixed * d_mixed.astype(jnp.float32), axis=-1, keepdims=True)
            d_scores = (probs * (d_probs - delta) * HEAD_DIM ** (-0.5)).astype(jnp.bfloat16)
            dqkv_ref[low:high, cols[0]] = dot_nn(d_scores, key_rows).astype(jnp.bfloat16)
            d_keys = dot_tn(d_scores, queries)
            d_values = dot_tn(probs_bf, d_mixed)
            if block > 0:
                past_keys, past_values = carried[head]
                dqkv_ref[key_low:low, cols[1]] = (past_keys + d_keys[:MOST]).astype(jnp.bfloat16)
                dqkv_ref[key_low:low, cols[2]] = (past_values + d_values[:MOST]).astype(
                    jnp.bfloat16
                )
                d_keys, d_values = d_keys[MOST:], d_values[MOST:]
            if block == blocks - 1:
                dqkv_ref[low:high, cols[1]] = d_keys.astype(jnp.bfloat16)
                dqkv_ref[low:high, cols[2]] = d_values.astype(jnp.bfloat16)
            carried[head] = (d_keys, d_values)
    for block in range(blocks):
        low, high = block * MOST, (block + 1) * MOST
        d_normed = dot_nt(dqkv_ref[low:high, :], w_ref[...]) * gain
        widened = x_ref[low:high, :].astype(jnp.float32)
        scale = scales[block]
        pull = jnp.mean(d_normed * widened, axis=-1, keepdims=True) * scale * scale * scale
        out_ref[low:high, :] = (d_normed * scale - widened * pull).astype(jnp.bfloat16)


SMEM_SPEC = pl.BlockSpec(memory_space=pltpu.SMEM)
VMEM_SPEC = pl.BlockSpec(memory_space=pltpu.VMEM)
ANY_SPEC = pl.BlockSpec(memory_space=pl.ANY)


def forward_term_of(lengths, gains, x, wq, wk, wv, wo):
    rows, wide, width = x.shape[1], x.shape[2], wq.shape[3]
    bf16 = jnp.bfloat16
    return pl.pallas_call(
        forward_kernel,
        out_shape=jax.ShapeDtypeStruct((rows, wide), bf16),
        in_specs=[SMEM_SPEC, VMEM_SPEC] + [ANY_SPEC] * 5,
        out_specs=VMEM_SPEC,
        scratch_shapes=[
            pltpu.VMEM((rows, wide), bf16),
            pltpu.VMEM((wide, 3 * width), bf16),
            pltpu.VMEM((width, wide), bf16),
            pltpu.VMEM((rows, 3 * width), bf16),
            pltpu.SemaphoreType.DMA((5,)),
        ],
        compiler_params=pltpu.CompilerParams(vmem_limit_bytes=VMEM_LIMIT),
        cost_estimate=pl.CostEstimate(
            flops=8 * rows * wide * width, bytes_accessed=8 * wide * (rows + width),
            transcendentals=rows * MOST,
        ),
        name="forward_section",
    )(lengths, gains, x, wq, wk, wv, wo)


def backward_terms_of(lengths, gains, x, c, wq, wk, wv, wo):
    rows, wide, width = x.shape[1], x.shape[2], wq.shape[3]
    bf16 = jnp.bfloat16
    return pl.pallas_call(
        backward_kernel,
        out_shape=(
            jax.ShapeDtypeStruct((rows, wide), bf16),
            jax.ShapeDtypeStruct((rows, width), bf16),
        ),
        in_specs=[SMEM_SPEC, VMEM_SPEC] + [ANY_SPEC] * 6,
        out_specs=(VMEM_SPEC, VMEM_SPEC),
        scratch_shapes=[
            pltpu.VMEM((rows, wide), bf16),
            pltpu.VMEM((rows, wide), bf16),
            pltpu.VMEM((wide, 3 * width), bf16),
            pltpu.VMEM((width, wide), bf16),
            pltpu.VMEM((rows, 3 * width), bf16),
            pltpu.VMEM((rows, 3 * width), bf16),
            pltpu.SemaphoreType.DMA((6,)),
        ],
        compiler_params=pltpu.CompilerParams(vmem_limit_bytes=VMEM_LIMIT),
        cost_estimate=pl.CostEstimate(
            flops=16 * rows * wide * width, bytes_accessed=8 * wide * (rows + width),
            transcendentals=rows * MOST,
        ),
        name="backward_section",
    )(lengths, gains, x, c, wq, wk, wv, wo)


def per_device(
    fwd_inputs,
    bwd_inputs,
    bwd_cotangent,
    fwd_lengths,
    bwd_lengths,
    norm_gains,
    query_weight,
    key_weight,
    value_weight,
    out_weight,
):
    row_count = fwd_inputs.shape[1]
    share_rows = row_count // lax.axis_size("tensor")
    row_start = lax.axis_index("tensor") * share_rows
    forward_in = fwd_inputs[0]
    cotangent = bwd_cotangent[0]
    forward_term = forward_term_of(
        fwd_lengths, norm_gains, fwd_inputs, query_weight, key_weight, value_weight, out_weight
    )
    backward_term, attended = backward_terms_of(
        bwd_lengths,
        norm_gains,
        bwd_inputs,
        bwd_cotangent,
        query_weight,
        key_weight,
        value_weight,
        out_weight,
    )
    weight_grad = dot_tn(attended, cotangent).astype(jnp.bfloat16)
    forward_rows = lax.dynamic_slice_in_dim(forward_in, row_start, share_rows, 0)
    cotangent_rows = lax.dynamic_slice_in_dim(cotangent, row_start, share_rows, 0)
    moved_section = chain_sums_along(forward_term, forward_rows, "tensor", "pipe")
    moved_grad = chain_sums_along(backward_term, cotangent_rows, "tensor", "pipe")
    mirrored = mirror_exchange(weight_grad, "pipe").astype(jnp.float32)
    return (moved_section[None], moved_grad[None], mirrored[None])


def solution(mesh):
    placed = (
        P("pipe", None, None),
        P("pipe", None, None),
        P("pipe", None, None),
        P("pipe", None),
        P("pipe", None),
        P(None, "pipe", None),
        P(None, "pipe", None, "tensor"),
        P(None, "pipe", None, "tensor"),
        P(None, "pipe", None, "tensor"),
        P(None, "pipe", "tensor", None),
    )
    return jax.shard_map(
        per_device,
        mesh=mesh,
        in_specs=placed,
        out_specs=(P("pipe", "tensor", None), P("pipe", "tensor", None), P("pipe", "tensor", None)),
        check_vma=False,
    )
```
